32 devices in a mesh: sen: 8 (over z, y), par: 4 (over x, core).
Axes of the slice: x: 2, y: 2, z: 4, core: 2. Of those that a mesh axis runs over, the one named last changes fastest.
Arguments:
- vectors: float32 [3, 256, 420], P(None, ('par', 'sen')), may hold values from -6 to 6
- kernel: float32 [160, 256, 420], P('sen', 'par'), may hold values from -0.01953125 to 0.01953125
- noise: float32 [160, 420], P('sen'), may hold values from 0.25 to 4
Outputs:
- products: float32 [3, 256, 420], P(None, ('par', 'sen'))
The draws below stay inside these ranges and needn't reach their ends.
All inputs are finite; a program needn't handle non-finite values.
Results may differ from the reference program's by a relative error of at most 0.0001.
Values sent between devices are 32-bit elements; how exact they have to be, the bound alone decides.
A program may use at most 128 MiB of HBM per device.

```python
import math
import jax
import jax.numpy as jnp
from jax import lax

NT = 420
SEN_DEV = 20
NV = 3
NSEN = 160
NPAR = 256
N_SEN = 8


def level_of(rng, shape, shards, smallest, top_value):
    gain, own = 1.0, jax.random.fold_in(rng, 6)
    for position, parts in shards:
        steps = jnp.exp(jax.random.uniform(jax.random.fold_in(own, position), (parts,), jnp.float32, smallest / len(shards), top_value / len(shards)))
        gain = gain * jnp.repeat(steps, shape[position] // parts).reshape([-1 if axis == position else 1 for axis in range(len(shape))])
    return gain


def bell_draw(own_key, extent, deviation, reach, split=(), dtype=jnp.bfloat16):
    result = deviation * jax.random.normal(own_key, extent, jnp.float32)
    if split:
        result = result * level_of(own_key, extent, split, -0.22, 0.18)
    return jnp.clip(result, -reach, reach).astype(dtype)


def setup_inputs(seed: int = 0) -> dict:
    splits = jax.random.split(jax.random.key(seed), 4)
    return {
        "vectors": bell_draw(splits[0], (NV, NPAR, NT), 1.0, 6.0, ((1, 32),), jnp.float32),
        "kernel": bell_draw(splits[1], (NSEN, NPAR, NT), (NPAR * NT) ** -0.5, 0.01953125, ((0, 8), (1, 4)), jnp.float32),
        "noise": jnp.clip(jnp.exp(math.log(4.0) - 2.7725887 * jax.random.uniform(splits[2], (NSEN, NT), jnp.float32) ** level_of(splits[2], (NSEN, NT), ((0, 8),), -0.2, 0.2)), 0.25, 4.0),
    }


def reference(vectors, kernel, noise):
    length = 2 * NT
    direction_spectrum = jnp.fft.rfft(vectors, n=length, axis=-1)
    blocks = kernel.reshape(N_SEN, SEN_DEV, NPAR, NT)
    noise_blocks = noise.reshape(N_SEN, SEN_DEV, NT)

    def step(carry, item):
        acc_re, acc_im = carry
        block, weights = item
        kernel_spectrum = jnp.fft.rfft(block, n=length, axis=-1)
        data_spectrum = jnp.einsum("qyn,hyn->hqn", kernel_spectrum, direction_spectrum)
        signal = jnp.fft.irfft(data_spectrum, n=length, axis=-1)[..., :NT]
        weighted_residual = weights[None] * signal
        weighted_spectrum = jnp.fft.rfft(weighted_residual, n=length, axis=-1)
        gradient_spectrum = jnp.einsum("gtc,rgc->rtc", jnp.conj(kernel_spectrum), weighted_spectrum)
        return (acc_re + jnp.real(gradient_spectrum), acc_im + jnp.imag(gradient_spectrum)), None

    init = (jnp.zeros((NV, NPAR, NT + 1), jnp.float32), jnp.zeros((NV, NPAR, NT + 1), jnp.float32))
    (acc_re, acc_im), _ = lax.scan(step, init, (blocks, noise_blocks))
    return jnp.fft.irfft(acc_re + 1j * acc_im, n=length, axis=-1)[..., :NT].astype(jnp.float32)
```

```python
import functools
import math

import jax
import jax.numpy as jnp
import numpy as np
from jax import lax
from jax.experimental import pallas as pl
from jax.experimental.pallas import tpu as pltpu
from jax.sharding import PartitionSpec as P

LANES = 128
MESH = pl.DeviceIdType.MESH


def round_up(value, step):
    return -(-value // step) * step


def make_tables(ntime):
    length = 2 * ntime
    nfreq = ntime + 1
    chunks = -(-nfreq // LANES)
    width = round_up(ntime, LANES)
    phase = np.arange(ntime)[:, None] * np.arange(nfreq)[None, :] % length
    angle = phase * (2.0 * math.pi / length)
    table = np.zeros((chunks, width, 2 * LANES), np.float64)
    factor = np.zeros((chunks, 1, 2 * LANES), np.float32)
    for c in range(chunks):
        freqs = np.arange(c * LANES, min((c + 1) * LANES, nfreq))
        table[c, :ntime, : len(freqs)] = np.cos(angle[:, freqs])
        table[c, :ntime, LANES : LANES + len(freqs)] = -np.sin(angle[:, freqs])
        weight = np.where((freqs == 0) | (freqs == ntime), 1.0, 2.0) / length
        factor[c, 0, : len(freqs)] = weight
        factor[c, 0, LANES : LANES + len(freqs)] = weight
    high = table.astype(np.float32).astype(jnp.bfloat16)
    low = (table - high.astype(np.float64)).astype(np.float32).astype(jnp.bfloat16)
    return high, low, factor


def split(x):
    high = x.astype(jnp.bfloat16)
    return high, (x - high.astype(jnp.float32)).astype(jnp.bfloat16)


def dot3(xh, xl, th, tl, transposed=False):
    dims = (((1,), (1 if transposed else 0,)), ((), ()))
    dot = functools.partial(lax.dot_general, dimension_numbers=dims, preferred_element_type=jnp.float32)
    return dot(xh, th) + dot(xh, tl) + dot(xl, th)


def body(n_sen, n_par, th, tl, fac, vec, kern, noise, out,
         xh, xl, spec, vg, vx, vhat, dhat, sig, sigr, what, ghat, gs, rs,
         vsend, vrecv, psend, precv, gsend, grecv):
    nvec, owned, ntime = vec.shape
    nsens, nsrc, _ = kern.shape
    chunks, width, _ = th.shape
    spad = round_up(nsens, 8)
    sen = lax.axis_index("sen")
    par = lax.axis_index("par")
    bits = n_par.bit_length() - 1
    partners = []
    for b in range(bits):
        w = 1 << b
        partners.append(par + (1 - 2 * ((par // w) % 2)) * w)

    barrier = pltpu.get_barrier_semaphore()
    for d in range(1, n_sen):
        pl.semaphore_signal(barrier, inc=1, device_id={"sen": (sen + d) % n_sen}, device_id_type=MESH)
    for p in partners:
        pl.semaphore_signal(barrier, inc=1, device_id={"par": p}, device_id_type=MESH)
    pl.semaphore_wait(barrier, n_sen - 1 + bits)

    def gather_copy(d):
        return pltpu.make_async_remote_copy(
            src_ref=vec, dst_ref=vg.at[sen], send_sem=vsend.at[d], recv_sem=vrecv.at[d],
            device_id={"sen": (sen + d) % n_sen}, device_id_type=MESH)

    for d in range(1, n_sen):
        gather_copy(d).start()
    vg[sen] = vec[...]

    tail = (ntime // LANES) * LANES
    if tail < width:
        xh[:, tail:] = jnp.zeros((nsens * nsrc, width - tail), jnp.bfloat16)
        xl[:, tail:] = jnp.zeros((nsens * nsrc, width - tail), jnp.bfloat16)
        vx[:, tail:] = jnp.zeros((nvec * nsrc, width - tail), jnp.float32)

    @pl.loop(0, nsens)
    def _(s):
        h, l = split(kern[s])
        rows = pl.ds(pl.multiple_of(s * nsrc, 16), nsrc)
        xh[rows, :ntime] = h
        xl[rows, :ntime] = l

    block = max(b for b in range(1, 11) if nsens % b == 0) * nsrc

    @pl.loop(0, chunks)
    def _(j):
        @pl.loop(0, nsens * nsrc // block)
        def _(m):
            rows = pl.ds(pl.multiple_of(m * block, 16), block)
            spec[j, rows, :] = dot3(xh[rows, :], xl[rows, :], th[j], tl[j])

    for d in range(1, n_sen):
        copy = gather_copy(d)
        copy.wait_send()
        copy.wait_recv()
    for o in range(n_sen):
        for v in range(nvec):
            vx[v * nsrc + o * owned : v * nsrc + (o + 1) * owned, :ntime] = vg[o, v]

    @pl.loop(0, chunks)
    def _(j):
        vhat[j] = dot3(*split(vx[...]), th[j], tl[j])

    dhat[...] = jnp.zeros(dhat.shape, jnp.float32)

    @pl.loop(0, chunks)
    def _(j):
        for s in range(nsens):
            rows = slice(s * nsrc, (s + 1) * nsrc)
            kr = spec[j, rows, :LANES]
            ki = spec[j, rows, LANES:]
            for v in range(nvec):
                vr = vhat[j, v * nsrc : (v + 1) * nsrc, :LANES]
                vi = vhat[j, v * nsrc : (v + 1) * nsrc, LANES:]
                row = slice(v * spad + s, v * spad + s + 1)
                dhat[j, row, :LANES] = jnp.sum(kr * vr - ki * vi, axis=0, keepdims=True)
                dhat[j, row, LANES:] = jnp.sum(kr * vi + ki * vr, axis=0, keepdims=True)

    signal = jnp.zeros((nvec * spad, width), jnp.float32)
    for j in range(chunks):
        signal = signal + dot3(*split(dhat[j] * fac[j]), th[j], tl[j], True)

    for b in range(bits):
        sig[b] = signal
        copy = pltpu.make_async_remote_copy(
            src_ref=sig.at[b], dst_ref=sigr.at[b], send_sem=psend.at[b], recv_sem=precv.at[b],
            device_id={"par": partners[b]}, device_id_type=MESH)
        copy.start()
        copy.wait()
        signal = sig[b] + sigr[b]

    sig[bits] = jnp.zeros((nvec * spad, width), jnp.float32)
    sig[bits] = signal
    for v in range(nvec):
        rows = slice(v * spad, v * spad + nsens)
        sig[bits, rows, :ntime] = sig[bits, rows, :ntime] * noise[...]

    @pl.loop(0, chunks)
    def _(j):
        what[j] = dot3(*split(sig[bits]), th[j], tl[j])

    step = math.gcd(nsrc, 32)

    @pl.loop(0, chunks)
    def _(j):
        @pl.loop(0, nsrc // step)
        def _(i):
            acc = [jnp.zeros((step, LANES), jnp.float32)] * (2 * nvec)
            for s in range(nsens):
                rows = pl.ds(pl.multiple_of(s * nsrc + i * step, 8), step)
                kr = spec[j, rows, :LANES]
                ki = spec[j, rows, LANES:]
                for v in range(nvec):
                    wr = what[j, v * spad + s : v * spad + s + 1, :LANES]
                    wi = what[j, v * spad + s : v * spad + s + 1, LANES:]
                    acc[2 * v] = acc[2 * v] + (kr * wr + ki * wi)
                    acc[2 * v + 1] = acc[2 * v + 1] + (kr * wi - ki * wr)
            for v in range(nvec):
                rows = pl.ds(pl.multiple_of(v * nsrc + i * step, 8), step)
                ghat[j, rows, :LANES] = acc[2 * v] * fac[j, :, :LANES]
                ghat[j, rows, LANES:] = acc[2 * v + 1] * fac[j, :, LANES:]

    grad = jnp.zeros((nvec * nsrc, width), jnp.float32)
    for j in range(chunks):
        grad = grad + dot3(*split(ghat[j]), th[j], tl[j], True)
    for o in range(n_sen):
        for v in range(nvec):
            gs[o, v * owned : (v + 1) * owned, :] = grad[v * nsrc + o * owned : v * nsrc + (o + 1) * owned]

    copies = []
    for d in range(1, n_sen):
        peer = (sen + d) % n_sen
        copies.append(pltpu.make_async_remote_copy(
            src_ref=gs.at[peer], dst_ref=rs.at[d], send_sem=gsend.at[d], recv_sem=grecv.at[d],
            device_id={"sen": peer}, device_id_type=MESH))
        copies[-1].start()
    total = gs[sen]
    for d in range(1, n_sen):
        copies[d - 1].wait()
        total = total + rs[d]
    for v in range(nvec):
        out[v] = total[v * owned : (v + 1) * owned, :ntime]


def per_device(n_sen, n_par, vectors, kernel, noise):
    nvec, owned, ntime = vectors.shape
    nsens, nsrc, _ = kernel.shape
    high, low, factor = make_tables(ntime)
    chunks, width, _ = high.shape
    spad = round_up(nsens, 8)
    bits = n_par.bit_length() - 1
    if n_par != 1 << bits:
        raise ValueError("par not 2^k")
    orow = round_up(nvec * owned, 8)
    f32, bf16 = jnp.float32, jnp.bfloat16
    vmem, dma = pltpu.VMEM, pltpu.SemaphoreType.DMA
    return pl.pallas_call(
        functools.partial(body, n_sen, n_par),
        out_shape=jax.ShapeDtypeStruct((nvec, owned, ntime), f32),
        in_specs=[pl.BlockSpec(memory_space=vmem)] * 6,
        out_specs=pl.BlockSpec(memory_space=vmem),
        scratch_shapes=[
            vmem((nsens * nsrc, width), bf16),
            vmem((nsens * nsrc, width), bf16),
            vmem((chunks, nsens * nsrc, 2 * LANES), f32),
            vmem((n_sen, nvec, owned, ntime), f32),
            vmem((nvec * nsrc, width), f32),
            vmem((chunks, nvec * nsrc, 2 * LANES), f32),
            vmem((chunks, nvec * spad, 2 * LANES), f32),
            vmem((bits + 1, nvec * spad, width), f32),
            vmem((max(bits, 1), nvec * spad, width), f32),
            vmem((chunks, nvec * spad, 2 * LANES), f32),
            vmem((chunks, nvec * nsrc, 2 * LANES), f32),
            vmem((n_sen, orow, width), f32),
            vmem((n_sen, orow, width), f32),
            dma((n_sen,)), dma((n_sen,)),
            dma((max(bits, 1),)), dma((max(bits, 1),)),
            dma((n_sen,)), dma((n_sen,)),
        ],
        compiler_params=pltpu.CompilerParams(
            collective_id=0, has_side_effects=True, vmem_limit_bytes=60 * 1024 * 1024),
    )(jnp.asarray(high), jnp.asarray(low), jnp.asarray(factor), vectors, kernel, noise)


def solution(mesh):
    n_sen, n_par = mesh.shape["sen"], mesh.shape["par"]
    return jax.shard_map(
        functools.partial(per_device, n_sen, n_par),
        mesh=mesh,
        in_specs=(P(None, ("par", "sen"), None), P("sen", "par", None), P("sen", None)),
        out_specs=P(None, ("par", "sen"), None),
        check_vma=False,
    )
```

```python
import functools
import math

import jax
import jax.numpy as jnp
import numpy as np
from jax import lax
from jax.experimental import pallas as pl
from jax.experimental.pallas import tpu as pltpu
from jax.sharding import PartitionSpec as P

LANES = 128
MESH = pl.DeviceIdType.MESH


def round_up(value, step):
    return -(-value // step) * step


def make_tables(ntime):
    length = 2 * ntime
    nfreq = ntime + 1
    chunks = -(-nfreq // LANES)
    width = round_up(ntime, LANES)
    phase = np.arange(ntime)[:, None] * np.arange(nfreq)[None, :] % length
    angle = phase * (2.0 * math.pi / length)
    table = np.zeros((chunks, width, 2 * LANES), np.float64)
    factor = np.zeros((chunks, 1, 2 * LANES), np.float32)
    for c in range(chunks):
        freqs = np.arange(c * LANES, min((c + 1) * LANES, nfreq))
        table[c, :ntime, : len(freqs)] = np.cos(angle[:, freqs])
        table[c, :ntime, LANES : LANES + len(freqs)] = -np.sin(angle[:, freqs])
        weight = np.where((freqs == 0) | (freqs == ntime), 1.0, 2.0) / length
        factor[c, 0, : len(freqs)] = weight
        factor[c, 0, LANES : LANES + len(freqs)] = weight
    high = table.astype(np.float32).astype(jnp.bfloat16)
    low = (table - high.astype(np.float64)).astype(np.float32).astype(jnp.bfloat16)
    return high, low, factor


def split(x):
    high = x.astype(jnp.bfloat16)
    return high, (x - high.astype(jnp.float32)).astype(jnp.bfloat16)


def dot3(xh, xl, th, tl, transposed=False):
    dims = (((1,), (1 if transposed else 0,)), ((), ()))
    dot = functools.partial(lax.dot_general, dimension_numbers=dims, preferred_element_type=jnp.float32)
    return dot(xh, th) + dot(xh, tl) + dot(xl, th)


def inner_factor(count):
    inner = 1
    while count % (inner * 2) == 0 and (inner * 2) ** 2 <= count:
        inner *= 2
    return inner


def sensor_block(nsens):
    return max(b for b in range(1, 11) if nsens % b == 0)


def body(n_sen, n_par, th_any, tl_any, fac, vec, kern_any, noise, out,
         th, tl, kern, weight, xh, xl, spec, vg, vx, vhat, dhat, half, halfr, sig, sigr, full, what, ghat, gs, rs1, hs, rs2,
         tsem, ksem, vsend, vrecv, wsend, wrecv, psend, precv, gsend, grecv, hsend, hrecv):
    nvec, owned, ntime = vec.shape
    nsens, nsrc, _ = kern.shape
    chunks, width, _ = th.shape
    spad = round_up(nsens, 8)
    inner = inner_factor(n_sen)
    outer = n_sen // inner
    sen = lax.axis_index("sen")
    par = lax.axis_index("par")
    row, col = sen // inner, sen % inner
    core = par % 2
    bits = n_par.bit_length() - 1
    partners = []
    for b in range(bits):
        w = 1 << b
        partners.append(par + (1 - 2 * ((par // w) % 2)) * w)

    def on_row(d):
        return ((row + d) % outer) * inner + col

    def on_col(e):
        return row * inner + (col + e) % inner

    peers = [{"sen": on_row(d)} for d in range(1, outer)] + [{"sen": on_col(e)} for e in range(1, inner)]
    peers += [{"par": p} for p in partners]
    barrier = pltpu.get_barrier_semaphore()
    for peer in peers:
        pl.semaphore_signal(barrier, inc=1, device_id=peer, device_id_type=MESH)

    block = sensor_block(nsens)
    pieces = nsens // block

    def kern_copy(m):
        part = pl.ds(m * block, block)
        return pltpu.make_async_copy(kern_any.at[part], kern.at[part], ksem.at[m])

    def table_copies(j):
        return [pltpu.make_async_copy(th_any.at[j], th.at[j], tsem.at[0, j]),
                pltpu.make_async_copy(tl_any.at[j], tl.at[j], tsem.at[1, j])]

    def start_tables(j):
        for copy in table_copies(j):
            copy.start()

    kern_copy(0).start()
    start_tables(0)
    for m in range(1, pieces):
        kern_copy(m).start()
    for j in range(1, chunks):
        start_tables(j)

    tail = (ntime // LANES) * LANES
    if tail < width:
        xh[:, tail:] = jnp.zeros((nsens * nsrc, width - tail), jnp.bfloat16)
        xl[:, tail:] = jnp.zeros((nsens * nsrc, width - tail), jnp.bfloat16)
        vx[:, tail:] = jnp.zeros((nvec * nsrc, width - tail), jnp.float32)
    dhat[...] = jnp.zeros(dhat.shape, jnp.float32)
    weight[...] = jnp.zeros(weight.shape, jnp.float32)
    weight[:nsens, :ntime] = noise[...]

    pl.semaphore_wait(barrier, len(peers))

    def row_copy(d):
        return pltpu.make_async_remote_copy(
            src_ref=vec, dst_ref=vg.at[sen], send_sem=vsend.at[d], recv_sem=vrecv.at[d],
            device_id={"sen": on_row(d)}, device_id_type=MESH)

    def col_copy(d, e):
        owner = ((row + outer - d) % outer) * inner + col
        return pltpu.make_async_remote_copy(
            src_ref=vec if d == 0 else vg.at[owner], dst_ref=vg.at[owner],
            send_sem=wsend.at[d, e], recv_sem=wrecv.at[d, e],
            device_id={"sen": on_col(e)}, device_id_type=MESH)

    def forward(d):
        if d:
            row_copy(d).wait_recv()
        for e in range(1, inner):
            col_copy(d, e).start()

    order = sorted(range(outer), key=lambda d: (abs(d - outer / 2), d))
    for d in order:
        if d:
            row_copy(d).start()
    forward(0)
    vg[sen] = vec[...]

    for m in range(pieces):
        kern_copy(m).wait()

        @pl.loop(m * block, (m + 1) * block)
        def _(s):
            h, l = split(kern[s])
            rows = pl.ds(pl.multiple_of(s * nsrc, 16), nsrc)
            xh[rows, :ntime] = h
            xl[rows, :ntime] = l

    pending = list(range(1, outer))
    for j in range(chunks):
        for copy in table_copies(j):
            copy.wait()

        @pl.loop(0, pieces)
        def _(m):
            rows = pl.ds(pl.multiple_of(m * block * nsrc, 16), block * nsrc)
            spec[j, rows, :] = dot3(xh[rows, :], xl[rows, :], th[j], tl[j])

        left = chunks - 1 - j
        count = -(-len(pending) // max(left, 1)) if j else 0
        for d in pending[:count]:
            forward(d)
        pending = pending[count:]
    for d in pending:
        forward(d)

    for d in range(1, outer):
        row_copy(d).wait_send()
    for d in range(outer):
        for e in range(1, inner):
            col_copy(d, e).wait()
    for o in range(n_sen):
        for v in range(nvec):
            vx[v * nsrc + o * owned : v * nsrc + (o + 1) * owned, :ntime] = vg[o, v]

    @pl.loop(0, chunks)
    def _(j):
        vhat[j] = dot3(*split(vx[...]), th[j], tl[j])

    @pl.loop(0, chunks)
    def _(j):
        for s in range(nsens):
            rows = slice(s * nsrc, (s + 1) * nsrc)
            kr = spec[j, rows, :LANES]
            ki = spec[j, rows, LANES:]
            for v in range(nvec):
                vr = vhat[j, v * nsrc : (v + 1) * nsrc, :LANES]
                vi = vhat[j, v * nsrc : (v + 1) * nsrc, LANES:]
                row = slice(v * spad + s, v * spad + s + 1)
                dhat[j, row, :LANES] = jnp.sum(kr * vr - ki * vi, axis=0, keepdims=True)
                dhat[j, row, LANES:] = jnp.sum(kr * vi + ki * vr, axis=0, keepdims=True)

    signal = jnp.zeros((nvec * spad, width), jnp.float32)
    for j in range(chunks):
        signal = signal + dot3(*split(dhat[j] * fac[j]), th[j], tl[j], True)

    def exchange(b, src, dst, k):
        copy = pltpu.make_async_remote_copy(
            src_ref=src, dst_ref=dst, send_sem=psend.at[k], recv_sem=precv.at[k],
            device_id={"par": partners[b]}, device_id_type=MESH)
        copy.start()
        copy.wait()

    half[0] = signal[:, : width // 2]
    half[1] = signal[:, width // 2 :]
    exchange(0, half.at[1 - core], halfr, bits)
    acc = half[core] + halfr[...]
    for b in range(1, bits):
        sig[b] = acc
        exchange(b, sig.at[b], sigr.at[b], b)
        acc = sig[b] + sigr[b]
    full[core] = acc
    exchange(0, full.at[core], full.at[core], 0)
    weighted = jnp.concatenate([full[0], full[1]], axis=1)
    weighted = weighted * jnp.concatenate([weight[...]] * nvec, axis=0)
    wh, wl = split(weighted)

    @pl.loop(0, chunks)
    def _(j):
        what[j] = dot3(wh, wl, th[j], tl[j])

    step = math.gcd(nsrc, 32)

    @pl.loop(0, chunks)
    def _(j):
        @pl.loop(0, nsrc // step)
        def _(i):
            acc = [jnp.zeros((step, LANES), jnp.float32)] * (2 * nvec)
            for s in range(nsens):
                rows = pl.ds(pl.multiple_of(s * nsrc + i * step, 8), step)
                kr = spec[j, rows, :LANES]
                ki = spec[j, rows, LANES:]
                for v in range(nvec):
                    wr = what[j, v * spad + s : v * spad + s + 1, :LANES]
                    wi = what[j, v * spad + s : v * spad + s + 1, LANES:]
                    acc[2 * v] = acc[2 * v] + (kr * wr + ki * wi)
                    acc[2 * v + 1] = acc[2 * v + 1] + (kr * wi - ki * wr)
            for v in range(nvec):
                rows = pl.ds(pl.multiple_of(v * nsrc + i * step, 8), step)
                ghat[j, rows, :LANES] = acc[2 * v] * fac[j, :, :LANES]
                ghat[j, rows, LANES:] = acc[2 * v + 1] * fac[j, :, LANES:]

    grad = jnp.zeros((nvec * nsrc, width), jnp.float32)
    for j in range(chunks):
        grad = grad + dot3(*split(ghat[j]), th[j], tl[j], True)
    for o in range(n_sen):
        for v in range(nvec):
            gs[o, v * owned : (v + 1) * owned, :] = grad[v * nsrc + o * owned : v * nsrc + (o + 1) * owned]

    def own_block(d, e):
        return ((row + d) % outer) * inner + (col + e) % inner

    def inner_copy(d, e):
        return pltpu.make_async_remote_copy(
            src_ref=gs.at[own_block(d, e)], dst_ref=rs1.at[d, e], send_sem=gsend.at[d, e], recv_sem=grecv.at[d, e],
            device_id={"sen": on_col(e)}, device_id_type=MESH)

    def outer_copy(d):
        return pltpu.make_async_remote_copy(
            src_ref=hs.at[d], dst_ref=rs2.at[d], send_sem=hsend.at[d], recv_sem=hrecv.at[d],
            device_id={"sen": on_row(d)}, device_id_type=MESH)

    for d in order:
        for e in range(1, inner):
            inner_copy(d, e).start()
    for d in order:
        part = gs[own_block(d, 0)]
        for e in range(1, inner):
            inner_copy(d, e).wait()
            part = part + rs1[d, e]
        if d:
            hs[d] = part
            outer_copy(d).start()
        else:
            total = part
    for d in order:
        if d:
            outer_copy(d).wait()
            total = total + rs2[d]
    for v in range(nvec):
        out[v] = total[v * owned : (v + 1) * owned, :ntime]


def per_device(n_sen, n_par, vectors, kernel, noise):
    nvec, owned, ntime = vectors.shape
    nsens, nsrc, _ = kernel.shape
    high, low, factor = make_tables(ntime)
    chunks, width, _ = high.shape
    spad = round_up(nsens, 8)
    bits = n_par.bit_length() - 1
    if bits < 1 or n_par != 1 << bits:
        raise ValueError("par not 2^k")
    orow = round_up(nvec * owned, 8)
    inner = inner_factor(n_sen)
    outer = n_sen // inner
    f32, bf16 = jnp.float32, jnp.bfloat16
    vmem, dma = pltpu.VMEM, pltpu.SemaphoreType.DMA
    return pl.pallas_call(
        functools.partial(body, n_sen, n_par),
        out_shape=jax.ShapeDtypeStruct((nvec, owned, ntime), f32),
        in_specs=[pl.BlockSpec(memory_space=pl.ANY if i in (0, 1, 4) else vmem) for i in range(6)],
        out_specs=pl.BlockSpec(memory_space=vmem),
        scratch_shapes=[
            vmem(high.shape, bf16),
            vmem(low.shape, bf16),
            vmem(kernel.shape, f32),
            vmem((spad, width), f32),
            vmem((nsens * nsrc, width), bf16),
            vmem((nsens * nsrc, width), bf16),
            vmem((chunks, nsens * nsrc, 2 * LANES), f32),
            vmem((n_sen, nvec, owned, ntime), f32),
            vmem((nvec * nsrc, width), f32),
            vmem((chunks, nvec * nsrc, 2 * LANES), f32),
            vmem((chunks, nvec * spad, 2 * LANES), f32),
            vmem((2, nvec * spad, width // 2), f32),
            vmem((nvec * spad, width // 2), f32),
            vmem((bits, nvec * spad, width // 2), f32),
            vmem((bits, nvec * spad, width // 2), f32),
            vmem((2, nvec * spad, width // 2), f32),
            vmem((chunks, nvec * spad, 2 * LANES), f32),
            vmem((chunks, nvec * nsrc, 2 * LANES), f32),
            vmem((n_sen, orow, width), f32),
            vmem((outer, inner, orow, width), f32),
            vmem((outer, orow, width), f32),
            vmem((outer, orow, width), f32),
            dma((2, chunks)), dma((nsens // sensor_block(nsens),)),
            dma((outer,)), dma((outer,)),
            dma((outer, inner)), dma((outer, inner)),
            dma((bits + 1,)), dma((bits + 1,)),
            dma((outer, inner)), dma((outer, inner)),
            dma((outer,)), dma((outer,)),
        ],
        compiler_params=pltpu.CompilerParams(
            collective_id=0, has_side_effects=True, vmem_limit_bytes=60 * 1024 * 1024),
    )(jnp.asarray(high), jnp.asarray(low), jnp.asarray(factor), vectors, kernel, noise)


def solution(mesh):
    n_sen, n_par = mesh.shape["sen"], mesh.shape["par"]
    return jax.shard_map(
        functools.partial(per_device, n_sen, n_par),
        mesh=mesh,
        in_specs=(P(None, ("par", "sen"), None), P("sen", "par", None), P("sen", None)),
        out_specs=P(None, ("par", "sen"), None),
        check_vma=False,
    )
```

```python
import functools
import math

import jax
import jax.numpy as jnp
import numpy as np
from jax import lax
from jax.experimental import pallas as pl
from jax.experimental.pallas import tpu as pltpu
from jax.sharding import PartitionSpec as P

LANES = 128
MESH = pl.DeviceIdType.MESH


def round_up(value, step):
    return -(-value // step) * step


def make_tables(ntime):
    length = 2 * ntime
    nfreq = ntime + 1
    chunks = -(-nfreq // LANES)
    width = round_up(ntime, LANES)
    phase = np.arange(ntime)[:, None] * np.arange(nfreq)[None, :] % length
    angle = phase * (2.0 * math.pi / length)
    table = np.zeros((chunks, width, 2 * LANES), np.float64)
    factor = np.zeros((chunks, 1, 2 * LANES), np.float32)
    for c in range(chunks):
        freqs = np.arange(c * LANES, min((c + 1) * LANES, nfreq))
        table[c, :ntime, : len(freqs)] = np.cos(angle[:, freqs])
        table[c, :ntime, LANES : LANES + len(freqs)] = -np.sin(angle[:, freqs])
        weight = np.where((freqs == 0) | (freqs == ntime), 1.0, 2.0) / length
        factor[c, 0, : len(freqs)] = weight
        factor[c, 0, LANES : LANES + len(freqs)] = weight
    high = table.astype(np.float32).astype(jnp.bfloat16)
    low = (table - high.astype(np.float64)).astype(np.float32).astype(jnp.bfloat16)
    return high, low, factor


def split(x):
    high = x.astype(jnp.bfloat16)
    return high, (x - high.astype(jnp.float32)).astype(jnp.bfloat16)


def packed_width(nvec, ntime):
    whole = ntime // LANES * LANES
    return nvec * whole + round_up(nvec * (ntime - whole), LANES)


def spans(v, nvec, ntime):
    whole = ntime // LANES * LANES
    rest = ntime - whole
    start = nvec * whole + v * rest
    pairs = [(slice(0, whole), slice(v * whole, (v + 1) * whole)), (slice(whole, ntime), slice(start, start + rest))]
    return [(a, b) for a, b in pairs if a.stop > a.start]


def stack(x):
    high, low = split(x)
    return jnp.concatenate([high, low, high], axis=1)


def dot(x, table):
    return jnp.dot(x, table, preferred_element_type=jnp.float32)


def dot3_transposed(xh, xl, th, tl):
    dims = (((1,), (1,)), ((), ()))
    dot = functools.partial(lax.dot_general, dimension_numbers=dims, preferred_element_type=jnp.float32)
    return dot(xh, th) + dot(xh, tl) + dot(xl, th)


def inner_factor(count):
    inner = 1
    while count % (inner * 2) == 0 and (inner * 2) ** 2 <= count:
        inner *= 2
    return inner


def sensor_block(nsens):
    return max(b for b in range(1, 11) if nsens % b == 0)


def body(n_sen, n_par, th_any, tl_any, fac, vec, kern_any, noise, out,
         tab, kern, weight, pack, x3, spec, vg, vx, vhat, dhat, half, halfr, sig, sigr, full, what, ghat, gs, rs1, hs, rs2,
         tsem, ksem, vsend, vrecv, wsend, wrecv, psend, precv, gsend, grecv, hsend, hrecv):
    nvec, owned, ntime = vec.shape
    nsens, nsrc, _ = kern.shape
    chunks, width, _ = th_any.shape
    spad = round_up(nsens, 8)
    inner = inner_factor(n_sen)
    outer = n_sen // inner
    sen = lax.axis_index("sen")
    par = lax.axis_index("par")
    row, col = sen // inner, sen % inner
    core = par % 2
    bits = n_par.bit_length() - 1
    partners = []
    for b in range(bits):
        w = 1 << b
        partners.append(par + (1 - 2 * ((par // w) % 2)) * w)

    def on_row(d):
        return ((row + d) % outer) * inner + col

    def on_col(e):
        return row * inner + (col + e) % inner

    peers = [{"sen": on_row(d)} for d in range(1, outer)] + [{"sen": on_col(e)} for e in range(1, inner)]
    peers += [{"par": p} for p in partners]
    barrier = pltpu.get_barrier_semaphore()
    for peer in peers:
        pl.semaphore_signal(barrier, inc=1, device_id=peer, device_id_type=MESH)

    block = sensor_block(nsens)
    pieces = nsens // block

    def kern_copy(m):
        part = pl.ds(m * block, block)
        return pltpu.make_async_copy(kern_any.at[part], kern.at[part], ksem.at[m])

    def table_copies(j):
        return [pltpu.make_async_copy(src.at[j], tab.at[j, pl.ds(i * width, width)], tsem.at[i, j])
                for i, src in enumerate((th_any, th_any, tl_any))]

    def start_tables(j):
        for copy in table_copies(j):
            copy.start()

    kern_copy(0).start()
    start_tables(0)
    for m in range(1, pieces):
        kern_copy(m).start()
    for j in range(1, chunks):
        start_tables(j)

    tail = (ntime // LANES) * LANES
    if tail < width:
        for i in range(3):
            x3[:, i * width + tail : (i + 1) * width] = jnp.zeros((nsens * nsrc, width - tail), jnp.bfloat16)
        vx[:, tail:] = jnp.zeros((nvec * nsrc, width - tail), jnp.float32)
    dhat[...] = jnp.zeros(dhat.shape, jnp.float32)
    pack[...] = jnp.zeros(pack.shape, jnp.float32)
    for v in range(nvec):
        for columns, place in spans(v, nvec, ntime):
            pack[:, place] = vec[v, :, columns]
    gs[...] = jnp.zeros(gs.shape, jnp.float32)
    weight[...] = jnp.zeros(weight.shape, jnp.float32)
    weight[:nsens, :ntime] = noise[...]

    pl.semaphore_wait(barrier, len(peers))

    def row_copy(d):
        return pltpu.make_async_remote_copy(
            src_ref=pack, dst_ref=vg.at[sen], send_sem=vsend.at[d], recv_sem=vrecv.at[d],
            device_id={"sen": on_row(d)}, device_id_type=MESH)

    def col_copy(d, e):
        owner = ((row + outer - d) % outer) * inner + col
        return pltpu.make_async_remote_copy(
            src_ref=pack if d == 0 else vg.at[owner], dst_ref=vg.at[owner],
            send_sem=wsend.at[d, e], recv_sem=wrecv.at[d, e],
            device_id={"sen": on_col(e)}, device_id_type=MESH)

    def forward(d):
        if d:
            row_copy(d).wait_recv()
        for e in range(1, inner):
            col_copy(d, e).start()

    order = sorted(range(outer), key=lambda d: (abs(d - outer / 2), d))
    for d in order:
        if d:
            row_copy(d).start()
    forward(0)
    vg[sen] = pack[...]

    for m in range(pieces):
        kern_copy(m).wait()

        @pl.loop(m * block, (m + 1) * block)
        def _(s):
            h, l = split(kern[s])
            rows = pl.ds(pl.multiple_of(s * nsrc, 16), nsrc)
            for i, part in enumerate((h, l, h)):
                x3[rows, i * width : i * width + ntime] = part

    pending = list(range(1, outer))
    for j in range(chunks):
        for copy in table_copies(j):
            copy.wait()

        @pl.loop(0, pieces)
        def _(m):
            rows = pl.ds(pl.multiple_of(m * block * nsrc, 16), block * nsrc)
            spec[j, rows, :] = dot(x3[rows, :], tab[j])

        left = chunks - 1 - j
        count = -(-len(pending) // max(left, 1)) if j else 0
        for d in pending[:count]:
            forward(d)
        pending = pending[count:]
    for d in pending:
        forward(d)

    for d in range(1, outer):
        row_copy(d).wait_send()
    for d in range(outer):
        for e in range(1, inner):
            col_copy(d, e).wait()
    for o in range(n_sen):
        for v in range(nvec):
            for columns, place in spans(v, nvec, ntime):
                vx[v * nsrc + o * owned : v * nsrc + (o + 1) * owned, columns] = vg[o, :, place]

    vstack = stack(vx[...])

    @pl.loop(0, chunks)
    def _(j):
        vhat[j] = dot(vstack, tab[j])

    @pl.loop(0, chunks)
    def _(j):
        for s in range(nsens):
            rows = slice(s * nsrc, (s + 1) * nsrc)
            kr = spec[j, rows, :LANES]
            ki = spec[j, rows, LANES:]
            for v in range(nvec):
                vr = vhat[j, v * nsrc : (v + 1) * nsrc, :LANES]
                vi = vhat[j, v * nsrc : (v + 1) * nsrc, LANES:]
                row = slice(v * spad + s, v * spad + s + 1)
                dhat[j, row, :LANES] = jnp.sum(kr * vr - ki * vi, axis=0, keepdims=True)
                dhat[j, row, LANES:] = jnp.sum(kr * vi + ki * vr, axis=0, keepdims=True)

    signal = jnp.zeros((nvec * spad, width), jnp.float32)
    for j in range(chunks):
        signal = signal + dot3_transposed(*split(dhat[j] * fac[j]), tab[j, :width], tab[j, 2 * width :])

    def exchange(b, src, dst, k):
        copy = pltpu.make_async_remote_copy(
            src_ref=src, dst_ref=dst, send_sem=psend.at[k], recv_sem=precv.at[k],
            device_id={"par": partners[b]}, device_id_type=MESH)
        copy.start()
        copy.wait()

    half[0] = signal[:, : width // 2]
    half[1] = signal[:, width // 2 :]
    exchange(0, half.at[1 - core], halfr, bits)
    acc = half[core] + halfr[...]
    for b in range(1, bits):
        sig[b] = acc
        exchange(b, sig.at[b], sigr.at[b], b)
        acc = sig[b] + sigr[b]
    full[core] = acc
    exchange(0, full.at[core], full.at[core], 0)
    weighted = jnp.concatenate([full[0], full[1]], axis=1)
    weighted = weighted * jnp.concatenate([weight[...]] * nvec, axis=0)
    wstack = stack(weighted)

    @pl.loop(0, chunks)
    def _(j):
        what[j] = dot(wstack, tab[j])

    step = math.gcd(nsrc, 32)

    @pl.loop(0, chunks)
    def _(j):
        @pl.loop(0, nsrc // step)
        def _(i):
            acc = [jnp.zeros((step, LANES), jnp.float32)] * (2 * nvec)
            for s in range(nsens):
                rows = pl.ds(pl.multiple_of(s * nsrc + i * step, 8), step)
                kr = spec[j, rows, :LANES]
                ki = spec[j, rows, LANES:]
                for v in range(nvec):
                    wr = what[j, v * spad + s : v * spad + s + 1, :LANES]
                    wi = what[j, v * spad + s : v * spad + s + 1, LANES:]
                    acc[2 * v] = acc[2 * v] + (kr * wr + ki * wi)
                    acc[2 * v + 1] = acc[2 * v + 1] + (kr * wi - ki * wr)
            for v in range(nvec):
                rows = pl.ds(pl.multiple_of(v * nsrc + i * step, 8), step)
                ghat[j, rows, :LANES] = acc[2 * v] * fac[j, :, :LANES]
                ghat[j, rows, LANES:] = acc[2 * v + 1] * fac[j, :, LANES:]

    grad = jnp.zeros((nvec * nsrc, width), jnp.float32)
    for j in range(chunks):
        grad = grad + dot3_transposed(*split(ghat[j]), tab[j, :width], tab[j, 2 * width :])
    for o in range(n_sen):
        for v in range(nvec):
            for columns, place in spans(v, nvec, ntime):
                gs[o, :, place] = grad[v * nsrc + o * owned : v * nsrc + (o + 1) * owned, columns]

    def own_block(d, e):
        return ((row + d) % outer) * inner + (col + e) % inner

    def inner_copy(d, e):
        return pltpu.make_async_remote_copy(
            src_ref=gs.at[own_block(d, e)], dst_ref=rs1.at[d, e], send_sem=gsend.at[d, e], recv_sem=grecv.at[d, e],
            device_id={"sen": on_col(e)}, device_id_type=MESH)

    def outer_copy(d):
        return pltpu.make_async_remote_copy(
            src_ref=hs.at[d], dst_ref=rs2.at[d], send_sem=hsend.at[d], recv_sem=hrecv.at[d],
            device_id={"sen": on_row(d)}, device_id_type=MESH)

    for d in order:
        for e in range(1, inner):
            inner_copy(d, e).start()
    for d in order:
        part = gs[own_block(d, 0)]
        for e in range(1, inner):
            inner_copy(d, e).wait()
            part = part + rs1[d, e]
        if d:
            hs[d] = part
            outer_copy(d).start()
        else:
            total = part
    for d in order:
        if d:
            outer_copy(d).wait()
            total = total + rs2[d]
    for v in range(nvec):
        for columns, place in spans(v, nvec, ntime):
            out[v, :, columns] = total[:, place]


def per_device(n_sen, n_par, vectors, kernel, noise):
    nvec, owned, ntime = vectors.shape
    nsens, nsrc, _ = kernel.shape
    high, low, factor = make_tables(ntime)
    chunks, width, _ = high.shape
    spad = round_up(nsens, 8)
    bits = n_par.bit_length() - 1
    if bits < 1 or n_par != 1 << bits:
        raise ValueError("par not 2^k")
    packed = packed_width(nvec, ntime)
    inner = inner_factor(n_sen)
    outer = n_sen // inner
    f32, bf16 = jnp.float32, jnp.bfloat16
    vmem, dma = pltpu.VMEM, pltpu.SemaphoreType.DMA
    return pl.pallas_call(
        functools.partial(body, n_sen, n_par),
        out_shape=jax.ShapeDtypeStruct((nvec, owned, ntime), f32),
        in_specs=[pl.BlockSpec(memory_space=pl.ANY if i in (0, 1, 4) else vmem) for i in range(6)],
        out_specs=pl.BlockSpec(memory_space=vmem),
        scratch_shapes=[
            vmem((chunks, 3 * width, 2 * LANES), bf16),
            vmem(kernel.shape, f32),
            vmem((spad, width), f32),
            vmem((owned, packed), f32),
            vmem((nsens * nsrc, 3 * width), bf16),
            vmem((chunks, nsens * nsrc, 2 * LANES), f32),
            vmem((n_sen, owned, packed), f32),
            vmem((nvec * nsrc, width), f32),
            vmem((chunks, nvec * nsrc, 2 * LANES), f32),
            vmem((chunks, nvec * spad, 2 * LANES), f32),
            vmem((2, nvec * spad, width // 2), f32),
            vmem((nvec * spad, width // 2), f32),
            vmem((bits, nvec * spad, width // 2), f32),
            vmem((bits, nvec * spad, width // 2), f32),
            vmem((2, nvec * spad, width // 2), f32),
            vmem((chunks, nvec * spad, 2 * LANES), f32),
            vmem((chunks, nvec * nsrc, 2 * LANES), f32),
            vmem((n_sen, owned, packed), f32),
            vmem((outer, inner, owned, packed), f32),
            vmem((outer, owned, packed), f32),
            vmem((outer, owned, packed), f32),
            dma((3, chunks)), dma((nsens // sensor_block(nsens),)),
            dma((outer,)), dma((outer,)),
            dma((outer, inner)), dma((outer, inner)),
            dma((bits + 1,)), dma((bits + 1,)),
            dma((outer, inner)), dma((outer, inner)),
            dma((outer,)), dma((outer,)),
        ],
        compiler_params=pltpu.CompilerParams(
            collective_id=0, has_side_effects=True, vmem_limit_bytes=60 * 1024 * 1024),
    )(jnp.asarray(high), jnp.asarray(low), jnp.asarray(factor), vectors, kernel, noise)


def solution(mesh):
    n_sen, n_par = mesh.shape["sen"], mesh.shape["par"]
    return jax.shard_map(
        functools.partial(per_device, n_sen, n_par),
        mesh=mesh,
        in_specs=(P(None, ("par", "sen"), None), P("sen", "par", None), P("sen", None)),
        out_specs=P(None, ("par", "sen"), None),
        check_vma=False,
    )
```

```python
import functools
import math

import jax
import jax.numpy as jnp
import numpy as np
from jax import lax
from jax.experimental import pallas as pl
from jax.experimental.pallas import tpu as pltpu
from jax.sharding import PartitionSpec as P

LANES = 128
MESH = pl.DeviceIdType.MESH


def round_up(value, step):
    return -(-value // step) * step


def make_tables(ntime):
    length = 2 * ntime
    nfreq = ntime + 1
    chunks = -(-nfreq // LANES)
    width = round_up(ntime, LANES)
    phase = np.arange(ntime)[:, None] * np.arange(nfreq)[None, :] % length
    angle = phase * (2.0 * math.pi / length)
    table = np.zeros((chunks, width, 2 * LANES), np.float64)
    factor = np.zeros((chunks, 1, 2 * LANES), np.float32)
    for c in range(chunks):
        freqs = np.arange(c * LANES, min((c + 1) * LANES, nfreq))
        table[c, :ntime, : len(freqs)] = np.cos(angle[:, freqs])
        table[c, :ntime, LANES : LANES + len(freqs)] = -np.sin(angle[:, freqs])
        weight = np.where((freqs == 0) | (freqs == ntime), 1.0, 2.0) / length
        factor[c, 0, : len(freqs)] = weight
        factor[c, 0, LANES : LANES + len(freqs)] = weight
    high = table.astype(np.float32).astype(jnp.bfloat16)
    low = (table - high.astype(np.float64)).astype(np.float32).astype(jnp.bfloat16)
    return high, low, factor


def split(x):
    high = x.astype(jnp.bfloat16)
    return high, (x - high.astype(jnp.float32)).astype(jnp.bfloat16)


def packed_width(nvec, ntime):
    whole = ntime // LANES * LANES
    return nvec * whole + round_up(nvec * (ntime - whole), LANES)


def spans(v, nvec, ntime):
    whole = ntime // LANES * LANES
    rest = ntime - whole
    start = nvec * whole + v * rest
    pairs = [(slice(0, whole), slice(v * whole, (v + 1) * whole)), (slice(whole, ntime), slice(start, start + rest))]
    return [(a, b) for a, b in pairs if a.stop > a.start]


def stack(x):
    high, low = split(x)
    return jnp.concatenate([high, low, high], axis=1)


def dot(x, table):
    return jnp.dot(x, table, preferred_element_type=jnp.float32)


def dot3_transposed(xh, xl, th, tl):
    dims = (((1,), (1,)), ((), ()))
    dot = functools.partial(lax.dot_general, dimension_numbers=dims, preferred_element_type=jnp.float32)
    return dot(xh, th) + dot(xh, tl) + dot(xl, th)


def inner_factor(count):
    inner = 1
    while count % (inner * 2) == 0 and (inner * 2) ** 2 <= count:
        inner *= 2
    return inner


def sensor_block(nsens):
    return max(b for b in range(1, 11) if nsens % b == 0)


def body(n_sen, n_par, th_any, tl_any, fac, vec, kern_any, noise, out,
         tab, kern, weight, pack, x3, spec, vg, vx, vhat, dhat, half, halfr, sig, sigr, full, what, ghat, gs, rs1, hs, rs2,
         tsem, ksem, vsend, vrecv, wsend, wrecv, psend, precv, gsend, grecv, hsend, hrecv):
    nvec, owned, ntime = vec.shape
    nsens, nsrc, _ = kern.shape
    chunks, width, _ = th_any.shape
    spad = round_up(nsens, 8)
    inner = inner_factor(n_sen)
    outer = n_sen // inner
    sen = lax.axis_index("sen")
    par = lax.axis_index("par")
    row, col = sen // inner, sen % inner
    core = par % 2
    bits = n_par.bit_length() - 1
    partners = []
    for b in range(bits):
        w = 1 << b
        partners.append(par + (1 - 2 * ((par // w) % 2)) * w)

    def on_row(d):
        return ((row + d) % outer) * inner + col

    def on_col(e):
        return row * inner + (col + e) % inner

    peers = [{"sen": on_row(d)} for d in range(1, outer)] + [{"sen": on_col(e)} for e in range(1, inner)]
    peers += [{"par": p} for p in partners]
    barrier = pltpu.get_barrier_semaphore()
    for peer in peers:
        pl.semaphore_signal(barrier, inc=1, device_id=peer, device_id_type=MESH)

    block = sensor_block(nsens)
    pieces = nsens // block

    def kern_copy(m):
        part = pl.ds(m * block, block)
        return pltpu.make_async_copy(kern_any.at[part], kern.at[part], ksem.at[m])

    def table_copies(j):
        return [pltpu.make_async_copy(src.at[j], tab.at[j, pl.ds(i * width, width)], tsem.at[i, j])
                for i, src in enumerate((th_any, th_any, tl_any))]

    def start_tables(j):
        for copy in table_copies(j):
            copy.start()

    kern_copy(0).start()
    start_tables(0)
    for m in range(1, pieces):
        kern_copy(m).start()
    for j in range(1, chunks):
        start_tables(j)

    tail = (ntime // LANES) * LANES
    if tail < width:
        for i in range(3):
            x3[:, i * width + tail : (i + 1) * width] = jnp.zeros((nsens * nsrc, width - tail), jnp.bfloat16)
        vx[:, tail:] = jnp.zeros((nvec * nsrc, width - tail), jnp.float32)
    dhat[...] = jnp.zeros(dhat.shape, jnp.float32)
    pack[...] = jnp.zeros(pack.shape, jnp.float32)
    for v in range(nvec):
        for columns, place in spans(v, nvec, ntime):
            pack[:, place] = vec[v, :, columns]
    gs[...] = jnp.zeros(gs.shape, jnp.float32)
    weight[...] = jnp.zeros(weight.shape, jnp.float32)
    weight[:nsens, :ntime] = noise[...]

    pl.semaphore_wait(barrier, len(peers))

    def row_copy(d):
        return pltpu.make_async_remote_copy(
            src_ref=pack, dst_ref=vg.at[sen], send_sem=vsend.at[d], recv_sem=vrecv.at[d],
            device_id={"sen": on_row(d)}, device_id_type=MESH)

    def col_copy(d, e):
        owner = ((row + outer - d) % outer) * inner + col
        return pltpu.make_async_remote_copy(
            src_ref=pack if d == 0 else vg.at[owner], dst_ref=vg.at[owner],
            send_sem=wsend.at[d, e], recv_sem=wrecv.at[d, e],
            device_id={"sen": on_col(e)}, device_id_type=MESH)

    def forward(d):
        if d:
            row_copy(d).wait_recv()
        for e in range(1, inner):
            col_copy(d, e).start()

    order = sorted(range(outer), key=lambda d: (abs(d - outer / 2), d))
    for d in order:
        if d:
            row_copy(d).start()
    forward(0)
    vg[sen] = pack[...]

    for m in range(pieces):
        kern_copy(m).wait()

        @pl.loop(m * block, (m + 1) * block)
        def _(s):
            h, l = split(kern[s])
            rows = pl.ds(pl.multiple_of(s * nsrc, 16), nsrc)
            for i, part in enumerate((h, l, h)):
                x3[rows, i * width : i * width + ntime] = part

    pending = [d for d in order if d]
    for j in range(chunks):
        for copy in table_copies(j):
            copy.wait()

        @pl.loop(0, pieces)
        def _(m):
            rows = pl.ds(pl.multiple_of(m * block * nsrc, 16), block * nsrc)
            spec[j, rows, :] = dot(x3[rows, :], tab[j])

        left = chunks - 1 - j
        count = -(-len(pending) // max(left, 1))
        for d in pending[:count]:
            forward(d)
        pending = pending[count:]
    for d in pending:
        forward(d)

    for d in range(1, outer):
        row_copy(d).wait_send()
    for d in range(outer):
        for e in range(1, inner):
            col_copy(d, e).wait()
    for o in range(n_sen):
        for v in range(nvec):
            for columns, place in spans(v, nvec, ntime):
                vx[v * nsrc + o * owned : v * nsrc + (o + 1) * owned, columns] = vg[o, :, place]

    vstack = stack(vx[...])

    @pl.loop(0, chunks)
    def _(j):
        vhat[j] = dot(vstack, tab[j])

    @pl.loop(0, chunks)
    def _(j):
        for s in range(nsens):
            rows = slice(s * nsrc, (s + 1) * nsrc)
            kr = spec[j, rows, :LANES]
            ki = spec[j, rows, LANES:]
            for v in range(nvec):
                vr = vhat[j, v * nsrc : (v + 1) * nsrc, :LANES]
                vi = vhat[j, v * nsrc : (v + 1) * nsrc, LANES:]
                row = slice(v * spad + s, v * spad + s + 1)
                dhat[j, row, :LANES] = jnp.sum(kr * vr - ki * vi, axis=0, keepdims=True)
                dhat[j, row, LANES:] = jnp.sum(kr * vi + ki * vr, axis=0, keepdims=True)

    signal = jnp.zeros((nvec * spad, width), jnp.float32)
    for j in range(chunks):
        signal = signal + dot3_transposed(*split(dhat[j] * fac[j]), tab[j, :width], tab[j, 2 * width :])

    def exchange(b, src, dst, k):
        copy = pltpu.make_async_remote_copy(
            src_ref=src, dst_ref=dst, send_sem=psend.at[k], recv_sem=precv.at[k],
            device_id={"par": partners[b]}, device_id_type=MESH)
        copy.start()
        copy.wait()

    half[0] = signal[:, : width // 2]
    half[1] = signal[:, width // 2 :]
    exchange(0, half.at[1 - core], halfr, bits)
    acc = half[core] + halfr[...]
    for b in range(1, bits):
        sig[b] = acc
        exchange(b, sig.at[b], sigr.at[b], b)
        acc = sig[b] + sigr[b]
    full[core] = acc
    exchange(0, full.at[core], full.at[core], 0)
    weighted = jnp.concatenate([full[0], full[1]], axis=1)
    weighted = weighted * jnp.concatenate([weight[...]] * nvec, axis=0)
    wstack = stack(weighted)

    @pl.loop(0, chunks)
    def _(j):
        what[j] = dot(wstack, tab[j])

    step = math.gcd(nsrc, 32)

    @pl.loop(0, chunks)
    def _(j):
        @pl.loop(0, nsrc // step)
        def _(i):
            acc = [jnp.zeros((step, LANES), jnp.float32)] * (2 * nvec)
            for s in range(nsens):
                rows = pl.ds(pl.multiple_of(s * nsrc + i * step, 8), step)
                kr = spec[j, rows, :LANES]
                ki = spec[j, rows, LANES:]
                for v in range(nvec):
                    wr = what[j, v * spad + s : v * spad + s + 1, :LANES]
                    wi = what[j, v * spad + s : v * spad + s + 1, LANES:]
                    acc[2 * v] = acc[2 * v] + (kr * wr + ki * wi)
                    acc[2 * v + 1] = acc[2 * v + 1] + (kr * wi - ki * wr)
            for v in range(nvec):
                rows = pl.ds(pl.multiple_of(v * nsrc + i * step, 8), step)
                ghat[j, rows, :LANES] = acc[2 * v] * fac[j, :, :LANES]
                ghat[j, rows, LANES:] = acc[2 * v + 1] * fac[j, :, LANES:]

    grad = jnp.zeros((nvec * nsrc, width), jnp.float32)
    for j in range(chunks):
        grad = grad + dot3_transposed(*split(ghat[j]), tab[j, :width], tab[j, 2 * width :])
    for o in range(n_sen):
        for v in range(nvec):
            for columns, place in spans(v, nvec, ntime):
                gs[o, :, place] = grad[v * nsrc + o * owned : v * nsrc + (o + 1) * owned, columns]

    def own_block(d, e):
        return ((row + d) % outer) * inner + (col + e) % inner

    def inner_copy(d, e):
        return pltpu.make_async_remote_copy(
            src_ref=gs.at[own_block(d, e)], dst_ref=rs1.at[d, e], send_sem=gsend.at[d, e], recv_sem=grecv.at[d, e],
            device_id={"sen": on_col(e)}, device_id_type=MESH)

    def outer_copy(d):
        return pltpu.make_async_remote_copy(
            src_ref=hs.at[d], dst_ref=rs2.at[d], send_sem=hsend.at[d], recv_sem=hrecv.at[d],
            device_id={"sen": on_row(d)}, device_id_type=MESH)

    for d in order:
        for e in range(1, inner):
            inner_copy(d, e).start()
    for d in order:
        part = gs[own_block(d, 0)]
        for e in range(1, inner):
            inner_copy(d, e).wait()
            part = part + rs1[d, e]
        if d:
            hs[d] = part
            outer_copy(d).start()
        else:
            total = part
    for d in order:
        if d:
            outer_copy(d).wait()
            total = total + rs2[d]
    for v in range(nvec):
        for columns, place in spans(v, nvec, ntime):
            out[v, :, columns] = total[:, place]


def per_device(n_sen, n_par, vectors, kernel, noise):
    nvec, owned, ntime = vectors.shape
    nsens, nsrc, _ = kernel.shape
    high, low, factor = make_tables(ntime)
    chunks, width, _ = high.shape
    spad = round_up(nsens, 8)
    bits = n_par.bit_length() - 1
    if bits < 1 or n_par != 1 << bits:
        raise ValueError("par not 2^k")
    packed = packed_width(nvec, ntime)
    inner = inner_factor(n_sen)
    outer = n_sen // inner
    f32, bf16 = jnp.float32, jnp.bfloat16
    vmem, dma = pltpu.VMEM, pltpu.SemaphoreType.DMA
    return pl.pallas_call(
        functools.partial(body, n_sen, n_par),
        out_shape=jax.ShapeDtypeStruct((nvec, owned, ntime), f32),
        in_specs=[pl.BlockSpec(memory_space=pl.ANY if i in (0, 1, 4) else vmem) for i in range(6)],
        out_specs=pl.BlockSpec(memory_space=vmem),
        scratch_shapes=[
            vmem((chunks, 3 * width, 2 * LANES), bf16),
            vmem(kernel.shape, f32),
            vmem((spad, width), f32),
            vmem((owned, packed), f32),
            vmem((nsens * nsrc, 3 * width), bf16),
            vmem((chunks, nsens * nsrc, 2 * LANES), f32),
            vmem((n_sen, owned, packed), f32),
            vmem((nvec * nsrc, width), f32),
            vmem((chunks, nvec * nsrc, 2 * LANES), f32),
            vmem((chunks, nvec * spad, 2 * LANES), f32),
            vmem((2, nvec * spad, width // 2), f32),
            vmem((nvec * spad, width // 2), f32),
            vmem((bits, nvec * spad, width // 2), f32),
            vmem((bits, nvec * spad, width // 2), f32),
            vmem((2, nvec * spad, width // 2), f32),
            vmem((chunks, nvec * spad, 2 * LANES), f32),
            vmem((chunks, nvec * nsrc, 2 * LANES), f32),
            vmem((n_sen, owned, packed), f32),
            vmem((outer, inner, owned, packed), f32),
            vmem((outer, owned, packed), f32),
            vmem((outer, owned, packed), f32),
            dma((3, chunks)), dma((nsens // sensor_block(nsens),)),
            dma((outer,)), dma((outer,)),
            dma((outer, inner)), dma((outer, inner)),
            dma((bits + 1,)), dma((bits + 1,)),
            dma((outer, inner)), dma((outer, inner)),
            dma((outer,)), dma((outer,)),
        ],
        compiler_params=pltpu.CompilerParams(
            collective_id=0, has_side_effects=True, vmem_limit_bytes=60 * 1024 * 1024),
    )(jnp.asarray(high), jnp.asarray(low), jnp.asarray(factor), vectors, kernel, noise)


def solution(mesh):
    n_sen, n_par = mesh.shape["sen"], mesh.shape["par"]
    return jax.shard_map(
        functools.partial(per_device, n_sen, n_par),
        mesh=mesh,
        in_specs=(P(None, ("par", "sen"), None), P("sen", "par", None), P("sen", None)),
        out_specs=P(None, ("par", "sen"), None),
        check_vma=False,
    )
```
